32 devices in a mesh: prow: 16 (over z, x, core), pcol: 2 (over y).
Axes of the slice: x: 2, y: 2, z: 4, core: 2. Of those that a mesh axis runs over, the one named last changes fastest.
Arguments:
- panel: bfloat16 [8192, 4096], P('prow', 'pcol'), may hold values from -0.09375 to 0.09375
- anc_inverse: bfloat16 [8192, 8192], P('prow', 'pcol'), may hold values from -6 to 6
- diag_inverse: bfloat16 [4096, 4096], P('prow', 'pcol'), may hold values from -6 to 6
- block_counts: int32 [16], replicated, may hold values from 0 to 4, as said below
Outputs:
- off_diag: bfloat16 [8192, 4096], P('prow', 'pcol')
- diag_block: float32 [4096, 4096], P('prow', 'pcol')
The draws below stay inside these ranges and needn't reach their ends.
Inputs may be any that keep to these rules, and one draw needn't show every extreme that they name: `block_counts`: they add up to exactly 32, and some grid row owns 4 blocks.
All inputs are finite; a program needn't handle non-finite values.
Results may differ from the reference program's by a relative error of at most 0.002.
Values may be sent and summed in bfloat16 or wider, within the bound.
No kernel may reach another device: no remote copies, remote signals or barrier semaphores. Data moves between devices by JAX's collectives and lax.ppermute only.
A program may use at most 128 MiB of HBM per device.

```python
import jax
import jax.numpy as jnp
from jax import lax

S = 4096
BLK = 128
BLK_DEV = 2
SLOT_ROWS = 512
ROWS = 4096
SLOTS = 8192
N_PROW = 16


def draw_block_counts(key, part):
    key_order = jax.random.fold_in(key, 11)
    key_amount = jax.random.fold_in(key, 12)
    ordering = jax.random.permutation(key_order, N_PROW)
    half_count = N_PROW // 2
    amounts = jax.random.randint(key_amount, (half_count,), 0, BLK_DEV + 1)
    amounts = amounts.at[0].set(BLK_DEV)
    result_counts = jnp.full((N_PROW,), BLK_DEV, jnp.int32)
    result_counts = result_counts.at[ordering[:half_count]].add(amounts)
    result_counts = result_counts.at[ordering[half_count:2 * half_count]].add(-amounts)
    return result_counts.astype(jnp.int32)


def draw_anc_inverse(key, part):
    key_values = jax.random.fold_in(key, 21)
    values = jnp.clip(jax.random.normal(key_values, (SLOTS, SLOTS), jnp.float32), -4.0, 4.0)
    return ((values + values.T) * 0.70710678).astype(jnp.bfloat16)


def steps_of(rng, extent, split, low, largest):
    def one(position, blocks):
        draws = jax.random.uniform(jax.random.fold_in(jax.random.fold_in(rng, 6), position), (blocks,), jnp.float32, low / len(split), largest / len(split))
        return jnp.repeat(jnp.exp(draws), extent[position] // blocks).reshape((-1,) + (1,) * (len(extent) - position - 1))

    loudness = one(*split[0])
    for cut in split[1:]:
        loudness = loudness * one(*cut)
    return loudness


def scatter_about(own_key, shape, scale, reach, pieces=(), kind=jnp.bfloat16):
    factor_of = steps_of(own_key, shape, pieces, -0.22, 0.18) if pieces else 1.0
    entries = jax.random.normal(own_key, shape, jnp.float32) * scale * factor_of
    return jnp.minimum(jnp.maximum(entries, -reach), reach).astype(kind)


def setup_inputs(seed: int = 0) -> dict:
    key_of = jax.random.split(jax.random.key(seed), 5)
    return {
        "panel": scatter_about(key_of[0], (SLOTS, S), ROWS ** -0.5, 0.09375, ((0, 16), (1, 2))),
        "anc_inverse": draw_anc_inverse(jax.random.fold_in(key_of[4], 71), 0),
        "diag_inverse": scatter_about(key_of[2], (S, S), 1.0, 6.0, ((0, 16), (1, 2))),
        "block_counts": draw_block_counts(jax.random.fold_in(key_of[4], 71), 0),
    }


def reference(panel, anc_inverse, diag_inverse, block_counts):
    slot_row = jnp.arange(SLOTS)
    owners_of = slot_row // SLOT_ROWS
    block_number = (slot_row % SLOT_ROWS) // BLK
    in_use = (block_number < block_counts[owners_of]).astype(jnp.float32)
    masked_panel = panel.astype(jnp.float32) * in_use[:, None]
    inverse_full = anc_inverse.astype(jnp.float32)
    product = jnp.dot(inverse_full, masked_panel, precision=lax.Precision.HIGHEST)
    off_diag = (-(in_use[:, None] * product)).astype(jnp.bfloat16)
    update = jnp.dot(masked_panel.T, off_diag.astype(jnp.float32), precision=lax.Precision.HIGHEST)
    diag_block = diag_inverse.astype(jnp.float32) - update
    return off_diag, diag_block
```

```python
import jax
import jax.numpy as jnp
from jax import lax
from jax.sharding import PartitionSpec as P

BLK = 128
CHUNKS = 2


def build(n_row, n_col):
    half = n_row // 2
    groups = [list(range(half)), list(range(half, n_row))]
    across = [(i, (i + half) % n_row) for i in range(n_row)]

    def spread(value):
        pieces = [value]
        for step in range(1, n_col):
            pairs = [(i, (i - step) % n_col) for i in range(n_col)]
            pieces.append(lax.ppermute(value, "pcol", pairs))
        return pieces

    def ordered(pieces, col):
        if n_col == 2:
            first = jnp.where(col == 0, pieces[0], pieces[1])
            second = jnp.where(col == 0, pieces[1], pieces[0])
            return [first, second]
        stacked = jnp.stack(pieces)
        return [stacked[(i - col) % n_col] for i in range(n_col)]

    def per_device(panel, anc_inverse, diag_inverse, block_counts):
        row = lax.axis_index("prow")
        col = lax.axis_index("pcol")
        slot_rows, width = panel.shape
        unit = diag_inverse.shape[0]
        units = width // unit
        own_count = block_counts[row]
        in_use = (jnp.arange(slot_rows) // BLK < own_count)[:, None]
        masked = jnp.where(in_use, panel, jnp.zeros_like(panel))
        gathered = lax.all_gather(masked, "prow", axis=0, tiled=True)
        inverse = jnp.concatenate(ordered(spread(anc_inverse), col), axis=1)

        low = row % half
        my_half = row // half
        half_rows = half * slot_rows
        mine = lax.dynamic_slice(
            gathered, (my_half * half_rows, lax.rem(low, units) * unit), (half_rows, unit)
        )
        everyone = spread(mine)
        if n_col > 2:
            stacked = jnp.stack(everyone)
            owner = low // units
            everyone = [stacked[(owner - col) % n_col], stacked[(owner + n_col // 2 - col) % n_col]]
        keeps_first = (my_half == col) if n_col == 2 else (my_half == 0)
        left = jnp.concatenate(everyone, axis=1)

        part = width // CHUNKS
        offs, blocks = [], []
        for i in range(CHUNKS):
            product = jnp.dot(
                inverse, gathered[:, i * part : (i + 1) * part], preferred_element_type=jnp.float32
            )
            off = jnp.where(in_use, -product, 0.0).astype(jnp.bfloat16)
            offs.append(off)
            half_off = lax.all_gather(
                off, "prow", axis=0, tiled=True, axis_index_groups=groups
            )
            share = lax.dot_general(
                left, half_off, (((0,), (0,)), ((), ())), preferred_element_type=jnp.float32
            )
            first, second = share[:unit], share[unit:]
            keep = jnp.where(keeps_first, first, second)
            give = jnp.where(keeps_first, second, first).astype(jnp.bfloat16)
            taken = lax.ppermute(give, "prow", across)
            before = diag_inverse[:, i * part : (i + 1) * part].astype(jnp.float32)
            blocks.append(before - (keep + taken.astype(jnp.float32)))
        return jnp.concatenate(offs, axis=1), jnp.concatenate(blocks, axis=1)

    return per_device


def solution(mesh):
    return jax.shard_map(
        build(mesh.shape["prow"], mesh.shape["pcol"]),
        mesh=mesh,
        in_specs=(P("prow", "pcol"), P("prow", "pcol"), P("prow", "pcol"), P()),
        out_specs=(P("prow", "pcol"), P("prow", "pcol")),
        check_vma=False,
    )
```
